256 devices in a mesh: seg: 8 (over x, core), tm: 32 (over y, z).
Axes of the slice: x: 4, y: 4, z: 8, core: 2. Of those that a mesh axis runs over, the one named last changes fastest.
Arguments:
- frames: bfloat16 [196608, 512], P(('seg', 'tm')), parts along dimension 0, may hold values from -6 to 6
- conv1_weight: bfloat16 [1024, 512], replicated, may hold values from -0.1875 to 0.1875
- conv1_gain: float32 [512], replicated, may hold values from 0.1 to 1.9
- conv2_weight: bfloat16 [1024, 512], replicated, may hold values from -0.1875 to 0.1875
- conv2_gain: float32 [512], replicated, may hold values from 0.1 to 1.9
- proj_gain: float32 [512], replicated, may hold values from 0.1 to 1.9
- proj_weight: bfloat16 [512, 1280], replicated, may hold values from -0.25 to 0.25
- mask_embed: float32 [1280], replicated, may hold values from -4 to 4
- attn_gain: float32 [1280], replicated, may hold values from 0.1 to 1.9
- qkv_weight: bfloat16 [1280, 3840], P('tm'), may hold values from -1 to 1
- out_weight: bfloat16 [1280, 1280], P('tm'), may hold values from -0.15625 to 0.15625
- span_starts: int32 [1536], P('seg'), parts along dimension 0, may hold values from 0 to 6127
- span_lengths: int32 [1536], P('seg'), parts along dimension 0, may hold values from 5 to 15
- valid_count: int32 [8], P('seg'), parts along dimension 0, may hold values from 1536 to 6144
Outputs:
- encoded: bfloat16 [49152, 1280], P(('seg', 'tm')), parts along dimension 0
The draws below stay inside these ranges and needn't reach their ends.
There are 8 independent parts, one for each index of `seg`. The reference program is written for one: setup_inputs(seed, part) draws one part's arguments, and reference() takes and returns one part's arrays. A program takes and returns all parts, laid end to end along the dimension named above; an argument that names none is the same for every part. Nothing has to cross between parts.
All inputs are finite; a program needn't handle non-finite values.
Results may differ from the reference program's by a relative error of at most 0.0085.
Values may be sent and summed in bfloat16 or wider, within the bound.
No kernel may reach another device: no remote copies, remote signals or barrier semaphores. Data moves between devices by JAX's collectives and lax.ppermute only.
A program may use at most 128 MiB of HBM per device.

```python
import jax
import jax.numpy as jnp
from jax import lax

C = 512
D = 1280
HEADS = 16
TOKENS = 6144
FRAMES = 24576
SPANS = 192


def draw_qkv_weight(key, part):
    normal_draw = jnp.clip(jax.random.normal(jax.random.fold_in(key, 101), (D, 3 * D), jnp.float32), -6.0, 6.0) * D ** (-0.5)
    query_cols = normal_draw[:, :D]
    key_cols = normal_draw[:, D:2 * D]
    value_cols = normal_draw[:, 2 * D:]
    query_cols = 1.6 * query_cols
    key_cols = 1.6 * key_cols
    return jnp.clip(jnp.concatenate([query_cols, key_cols, value_cols], axis=1), -1.0, 1.0).astype(jnp.bfloat16)


def plant(drawn, own_key, smallest, top_value):
    extent = drawn.shape
    index_at = [jax.random.randint(jax.random.fold_in(own_key, axis), (), 0, extent[axis]) for axis in range(len(extent))]
    drawn = drawn.at[tuple(index_at)].set(smallest)
    longest = extent.index(max(extent))
    index_at[longest] = (index_at[longest] + 1) % extent[longest]
    return drawn.at[tuple(index_at)].set(top_value)


def block_levels(key, shape, shards, least, largest):
    level, own = 1.0, jax.random.fold_in(key, 6)
    for axis_at, shards_of in shards:
        heights = jnp.exp(jax.random.uniform(jax.random.fold_in(own, axis_at), (shards_of,), jnp.float32, least / len(shards), largest / len(shards)))
        level = level * jnp.repeat(heights, shape[axis_at] // shards_of).reshape([-1 if axis == axis_at else 1 for axis in range(len(shape))])
    return level


def noise(key, shape, scale, bound, cuts=(), kind=jnp.bfloat16):
    drawn = jax.random.normal(key, shape, jnp.float32) * scale
    if len(cuts) > 0:
        drawn = block_levels(key, shape, cuts, -0.22, 0.18) * drawn
    return jnp.clip(drawn, min=-bound, max=bound).astype(kind)


def setup_inputs(seed: int = 0, part: int = 0) -> dict:
    keys = jax.random.split(jax.random.key(seed), 15)
    part_keys = jax.random.split(jax.random.fold_in(keys[14], part), 15)
    frames = noise(part_keys[0], (FRAMES, C), 1.0, 6.0, ((0, 32),))
    conv1_weight = noise(keys[1], (2 * C, C), (2 * C) ** -0.5, 0.1875)
    conv1_gain = jnp.clip(1.0 + 0.18 * jax.random.normal(keys[2], (C,), jnp.float32), 0.1, 1.9)
    conv2_weight = noise(keys[3], (2 * C, C), (2 * C) ** -0.5, 0.1875)
    conv2_gain = jnp.clip(1.0 + 0.18 * jax.random.normal(keys[4], (C,), jnp.float32), 0.1, 1.9)
    proj_gain = jnp.clip(1.0 + 0.18 * jax.random.normal(keys[5], (C,), jnp.float32), 0.1, 1.9)
    proj_weight = noise(keys[6], (C, D), C ** -0.5, 0.25)
    mask_embed = noise(keys[7], (D,), 1.0, 4.0, (), jnp.float32)
    attn_gain = jnp.clip(1.0 + 0.18 * jax.random.normal(keys[8], (D,), jnp.float32), 0.1, 1.9)
    qkv_weight = draw_qkv_weight(jax.random.fold_in(keys[14], 71), part)
    out_weight = noise(keys[10], (D, D), D ** -0.5, 0.15625, ((0, 32),))
    span_starts = plant(jax.random.randint(part_keys[11], (SPANS,), 0, TOKENS - 16), jax.random.fold_in(part_keys[11], 1), 0, (TOKENS - 16) - 1).astype(jnp.int32)
    span_lengths = plant(jax.random.randint(part_keys[12], (SPANS,), 5, 16), jax.random.fold_in(part_keys[12], 1), 5, 15).astype(jnp.int32)
    valid_count = jax.random.randint(part_keys[13], (1,), TOKENS // 4, TOKENS + 1).astype(jnp.int32)
    return {"frames": frames, "conv1_weight": conv1_weight, "conv1_gain": conv1_gain, "conv2_weight": conv2_weight, "conv2_gain": conv2_gain, "proj_gain": proj_gain, "proj_weight": proj_weight, "mask_embed": mask_embed, "attn_gain": attn_gain, "qkv_weight": qkv_weight, "out_weight": out_weight, "span_starts": span_starts, "span_lengths": span_lengths, "valid_count": valid_count}


epsilon = 1e-05

def layer_norm(values, gain_row):
    center = values - lax.optimization_barrier(jnp.mean(values, axis=-1, keepdims=True))
    spread = lax.optimization_barrier(jnp.mean(center * center, axis=-1, keepdims=True))
    return center * lax.rsqrt(spread + epsilon) * gain_row

def conv_block(inputs, weight, gain_row):
    stacked = inputs.reshape(inputs.shape[0] // 2, 2 * inputs.shape[1])
    mixed = jnp.dot(stacked, weight, preferred_element_type=jnp.float32)
    return jax.nn.gelu(layer_norm(mixed, gain_row), approximate=False).astype(jnp.bfloat16)

def reference(frames, conv1_weight, conv1_gain, conv2_weight, conv2_gain, proj_gain, proj_weight, mask_embed, attn_gain, qkv_weight, out_weight, span_starts, span_lengths, valid_count):
    first_conv = conv_block(frames, conv1_weight, conv1_gain)
    second_conv = conv_block(first_conv, conv2_weight, conv2_gain)
    normed = layer_norm(second_conv.astype(jnp.float32), proj_gain).astype(jnp.bfloat16)
    projected = jnp.dot(normed, proj_weight, preferred_element_type=jnp.float32)
    positions = jnp.arange(TOKENS, dtype=jnp.int32)
    span_ends = span_starts + span_lengths
    covered = jnp.any((positions[:, None] >= span_starts[None, :]) & (positions[:, None] < span_ends[None, :]), axis=1)
    valid_upto = valid_count[0]
    live_rows = positions < valid_upto
    residual = jnp.where(covered[:, None], mask_embed[None, :], projected)
    residual = jnp.where(live_rows[:, None], residual, 0.0)
    attn_in = layer_norm(residual, attn_gain).astype(jnp.bfloat16)
    joined_rows = jnp.dot(attn_in, qkv_weight, preferred_element_type=jnp.float32).astype(jnp.bfloat16)
    per_head = D // HEADS
    queries = joined_rows[:, :D].reshape(TOKENS, HEADS, per_head).transpose(1, 0, 2)
    keys_all = joined_rows[:, D:2 * D].reshape(TOKENS, HEADS, per_head).transpose(1, 0, 2)
    values_all = joined_rows[:, 2 * D:].reshape(TOKENS, HEADS, per_head).transpose(1, 0, 2)
    score_scale = per_head ** (-0.5)

    def one_head(operands):
        head_query, head_key, head_value = operands
        scores = lax.dot_general(head_query, head_key, (((1,), (1,)), ((), ())), preferred_element_type=jnp.float32) * score_scale
        scores = jnp.where(live_rows[None, :], scores, -jnp.inf)
        row_peak = lax.optimization_barrier(jnp.max(scores, axis=1, keepdims=True))
        weights = jnp.exp(scores - row_peak)
        running = lax.optimization_barrier(jnp.sum(weights, axis=1, keepdims=True))
        mixed = jnp.dot(weights.astype(jnp.bfloat16), head_value, preferred_element_type=jnp.float32)
        return (mixed / running).astype(jnp.bfloat16)
    heads_out = lax.map(one_head, (queries, keys_all, values_all))
    merged = heads_out.transpose(1, 0, 2).reshape(TOKENS, D)
    attended = jnp.dot(merged, out_weight, preferred_element_type=jnp.float32)
    return jnp.where(live_rows[:, None], residual + attended, 0.0).astype(jnp.bfloat16)
```

```python
import functools

import jax
import jax.numpy as jnp
from jax import lax
from jax.experimental import pallas as pl
from jax.experimental.pallas import tpu as pltpu
from jax.sharding import PartitionSpec as P

HEADS = 16
NY, NZ = 4, 8
ROWS = 192
GROUP = ROWS * NZ
C = 512
D = 1280
HD = 80
PAIR = 2 * HD
EPS = 1e-05
LOG2E = 1.4426950408889634
LOW = -1e30
f32, bf16 = jnp.float32, jnp.bfloat16
VM = pl.BlockSpec(memory_space=pltpu.VMEM)
SM = pl.BlockSpec(memory_space=pltpu.SMEM)


def norm(values, gain_row):
    center = values - jnp.mean(values, axis=-1, keepdims=True)
    spread = jnp.mean(center * center, axis=-1, keepdims=True)
    return center * lax.rsqrt(spread + EPS) * gain_row


def gelu(v):
    return 0.5 * v * (1.0 + lax.erf(v * 0.7071067811865476))


def mm(a, b):
    return jnp.dot(a, b, preferred_element_type=f32)


def residual_of(normed, proj_weight, embed, starts, lengths, position, valid):
    projected = mm(normed, proj_weight)
    hit = (position >= starts) & (position < starts + lengths)
    covered = jnp.max(hit.astype(jnp.int32), axis=1, keepdims=True) > 0
    residual = jnp.where(covered, embed, projected)
    return jnp.where(position < valid, residual, 0.0)


def conv_kernel(scal, x_ref, w1_ref, g1_ref, w2_ref, g2_ref, pg_ref, pw_ref, me_ref, st_ref, ln_ref,
                normed_ref, res_ref, a_ref, b_ref):
    def pairs(inputs, w_ref, rows):
        left = mm(inputs, w_ref[:C, :])
        right = mm(inputs, w_ref[C:, :])
        parts = []
        for i in range(C // 128):
            a_ref[i, pl.ds(0, 2 * rows), :] = left[:, 128 * i:128 * i + 128]
            b_ref[i, pl.ds(0, 2 * rows), :] = right[:, 128 * i:128 * i + 128]
            parts.append(a_ref[i, pl.ds(0, rows, stride=2), :] + b_ref[i, pl.ds(1, rows, stride=2), :])
        return jnp.concatenate(parts, axis=1)

    first = gelu(norm(pairs(x_ref[...], w1_ref, 2 * ROWS), g1_ref[...])).astype(bf16)
    second = gelu(norm(pairs(first, w2_ref, ROWS), g2_ref[...])).astype(bf16)
    normed = norm(second.astype(f32), pg_ref[...]).astype(bf16)
    normed_ref[...] = normed
    position = (scal[0] * NZ + scal[1]) * ROWS + lax.broadcasted_iota(jnp.int32, (ROWS, 1), 0)
    res_ref[...] = residual_of(normed, pw_ref[...], me_ref[...], st_ref[...], ln_ref[...], position, scal[2])


def qkv_kernel(scal, idx, x_ref, pw_ref, me_ref, ag_ref, st_ref, ln_ref, w_ref, q_ref, kv_ref, ws_ref):
    step = pl.program_id(0)
    block = 2 * ROWS

    @pl.when(step == 0)
    def _():
        for r in range(NY * NZ):
            ws_ref[40 * r:40 * r + 40, :] = w_ref[idx[r]]

    row = lax.broadcasted_iota(jnp.int32, (block, 1), 0)
    chunk = step * 2 + (row >= ROWS).astype(jnp.int32)
    z = (scal[1] + chunk) & (NZ - 1)
    position = scal[0] * GROUP + z * ROWS + row - jnp.where(row >= ROWS, ROWS, 0)
    residual = residual_of(x_ref[...], pw_ref[...], me_ref[...], st_ref[...], ln_ref[...], position, scal[2])
    attn_in = norm(residual, ag_ref[...]).astype(bf16)
    joined = mm(attn_in, ws_ref[...]).astype(bf16)
    scaled = joined[:, :PAIR].astype(f32) * (LOG2E * HD ** -0.5)
    hi = scaled.astype(bf16)
    lo = (scaled - hi.astype(f32)).astype(bf16)
    one = jnp.ones((block, 1), bf16)
    pad = jnp.zeros((block, 95), bf16)
    parts = []
    for h in range(2):
        parts += [hi[:, h * HD:h * HD + HD], lo[:, h * HD:h * HD + HD], one, pad]
    q_ref[...] = jnp.concatenate(parts, axis=1)
    kv_ref[...] = joined[:, PAIR:].astype(f32).T.astype(bf16)


def attend_kernel(offsets, first, last, *refs):
    count = len(offsets)
    scal, q_ref = refs[:2]
    kv_refs = refs[2:2 + count]
    rest = refs[2 + count:]
    if first:
        out_ref, kk, vv = rest
        prev = None
    else:
        prev, out_ref, kk, vv = rest
    block = 2 * ROWS
    valid = scal[2]
    base = [((scal[0] + d) & (NY - 1)) * GROUP for d in offsets]

    @pl.when(pl.program_id(0) == 0)
    def _():
        col = lax.broadcasted_iota(jnp.int32, (16, GROUP), 1)
        row = lax.broadcasted_iota(jnp.int32, (16, GROUP), 0)
        part = col // ROWS
        place = ((scal[1] + part) & (NZ - 1)) * ROWS + col - part * ROWS
        for c in range(count):
            bias = jnp.where((row == 0) & (base[c] + place >= valid), LOW, 0.0).astype(bf16)
            for h in range(2):
                keys = kv_refs[c][h * HD:h * HD + HD, :]
                kk[c, h, 0:HD, :] = keys
                kk[c, h, HD:2 * HD, :] = keys
                kk[c, h, 2 * HD:2 * HD + 16, :] = bias
                kk[c, h, 2 * HD + 16:, :] = jnp.zeros((80, GROUP), bf16)
                vv[c, h, 0:HD, :] = kv_refs[c][PAIR + h * HD:PAIR + h * HD + HD, :]
                vv[c, h, HD:HD + 16, :] = jnp.where(row == 0, 1.0, 0.0).astype(bf16)
                vv[c, h, HD + 16:, :] = jnp.zeros((32, GROUP), bf16)

    lane = lax.broadcasted_iota(jnp.int32, (block, 128), 1)
    if first:
        state = [jnp.where(lane == HD + 1, LOW, 0.0)] * 2
    else:
        state = [prev[:, h * 128:h * 128 + 128] for h in range(2)]

    def chunk_step(c, state):
        new = []
        for h in range(2):
            scores = mm(q_ref[:, h * 256:h * 256 + 256], kk[c, h])
            old = state[h][:, HD + 1:HD + 2]
            peak = jnp.maximum(old, jnp.max(scores, axis=1, keepdims=True))
            weights = jnp.exp2(scores - peak).astype(bf16)
            mixed = lax.dot_general(weights, vv[c, h], (((1,), (1,)), ((), ())), preferred_element_type=f32)
            acc = state[h] * jnp.exp2(old - peak) + mixed
            new.append(jnp.where(lane == HD + 1, peak, acc))
        return new

    for c in range(count):
        state = lax.cond(base[c] < valid, functools.partial(chunk_step, c), lambda s: s, state)
    if last:
        done = [(state[h] / state[h][:, HD:HD + 1])[:, :HD] for h in range(2)]
        both = jnp.concatenate(done, axis=1)
        for b in range(2):
            rows = both[b * ROWS:b * ROWS + ROWS]
            out_ref[b, 0:ROWS, :] = rows[:, :128].astype(bf16)
            tail = rows[:, 128:]
            packed = jnp.concatenate([tail[48 * i:48 * i + 48] for i in range(4)], axis=1)
            out_ref[b, ROWS:, :] = packed.astype(bf16)
    else:
        for h in range(2):
            out_ref[:, h * 128:h * 128 + 128] = state[h]


def attend(offsets, first, last, scal, queries, chunks, state):
    count = len(offsets)
    block = 2 * ROWS
    kv_spec = pl.BlockSpec((2 * PAIR, GROUP), lambda i: (0, 0))
    state_spec = pl.BlockSpec((block, 256), lambda i: (i, 0))
    in_specs = [SM, pl.BlockSpec((block, 512), lambda i: (i, 0))] + [kv_spec] * count
    args = [scal, queries] + list(chunks)
    if not first:
        in_specs.append(state_spec)
        args.append(state)
    if last:
        out_shape = jax.ShapeDtypeStruct((NZ, 240, 128), bf16)
        out_spec = pl.BlockSpec((2, 240, 128), lambda i: (i, 0, 0))
    else:
        out_shape = jax.ShapeDtypeStruct((GROUP, 256), f32)
        out_spec = state_spec
    return pl.pallas_call(
        functools.partial(attend_kernel, offsets, first, last),
        grid=(GROUP // block,),
        in_specs=in_specs,
        out_specs=out_spec,
        out_shape=out_shape,
        scratch_shapes=[pltpu.VMEM((count, 2, 256, GROUP), bf16), pltpu.VMEM((count, 2, 128, GROUP), bf16)],
        cost_estimate=pl.CostEstimate(
            flops=count * 4 * GROUP * GROUP * 512, bytes_accessed=count * 2 * PAIR * GROUP * 2,
            transcendentals=count * 2 * GROUP * GROUP),
        name="attend_%d_%d" % (count, int(last)),
    )(*args)


def out_kernel(scal, idx, res_ref, m_ref, ow_ref, out_ref, os_ref):
    for r in range(NY * NZ):
        os_ref[40 * r:40 * r + 40, :] = ow_ref[idx[r]]
    total = res_ref[...]
    for j in range(NZ):
        tail = m_ref[j, ROWS:, :]
        tail = jnp.concatenate([tail[:, 32 * i:32 * i + 32] for i in range(4)], axis=0)
        merged = jnp.concatenate([m_ref[j, :ROWS, :], tail], axis=1)
        start = pl.multiple_of(((scal[1] - j) & (NZ - 1)) * PAIR, PAIR)
        total = total + mm(merged, os_ref[pl.ds(start, PAIR), :])
    position = (scal[0] * NZ + scal[1]) * ROWS + lax.broadcasted_iota(jnp.int32, (ROWS, 1), 0)
    out_ref[...] = jnp.where(position < scal[2], total, 0.0).astype(bf16)


def z_perm(shift):
    return [(y * NZ + z, y * NZ + (z + shift) % NZ) for y in range(NY) for z in range(NZ)]


def y_perm(shift):
    return [(y * NZ + z, ((y + shift) % NY) * NZ + z) for y in range(NY) for z in range(NZ)]


def seg_perm(shift):
    return [(s, (s + shift) % 8) for s in range(8)]


def fetch_perm(k):
    return [
        (s * 32 + ((y + k) % NY) * NZ + (z + s) % NZ, s * 32 + y * NZ + z)
        for s in range(8) for y in range(NY) for z in range(NZ)
    ]


def share(blocks):
    got = jnp.stack([lax.ppermute(b, ("seg", "tm"), fetch_perm(k)) for k, b in enumerate(blocks)])
    ahead = lax.ppermute(got, "seg", seg_perm(-2))
    behind = lax.ppermute(got, "seg", seg_perm(2))
    across = lax.ppermute(got, "seg", seg_perm(4))
    mine = jnp.concatenate([got, ahead, across, behind])
    other = lax.ppermute(mine, "seg", [(s, s ^ 1) for s in range(8)])
    return jnp.concatenate([mine, other])


def local(frames, conv1_weight, conv1_gain, conv2_weight, conv2_gain, proj_gain, proj_weight, mask_embed,
          attn_gain, qkv_weight, out_weight, span_starts, span_lengths, valid_count):
    s = lax.axis_index("seg")
    t = lax.axis_index("tm")
    y, z = t // NZ, t % NZ
    scal = jnp.stack([y, z, valid_count[0]]).astype(jnp.int32)
    block_at = jnp.arange(NY * NZ, dtype=jnp.int32)
    k_of = (block_at // NZ - y) % NY
    s_of = (block_at % NZ - z) % NZ
    x_of = (s_of // 2 - s // 2) % 4
    c_of = (s_of + s) % 2
    idx = (c_of * 16 + x_of * 4 + k_of).astype(jnp.int32)

    target = (z - s) % NZ
    columns = lax.dynamic_slice_in_dim(qkv_weight.reshape(40, 3, NZ, PAIR), target, 1, axis=2)
    columns = columns.reshape(40, 3 * PAIR)
    w_blocks = share([columns] * NY)

    row = lambda v: v.reshape(1, -1)
    spans = (row(span_starts), row(span_lengths))
    normed, residual = pl.pallas_call(
        conv_kernel,
        in_specs=[SM] + [VM] * 10,
        out_specs=(VM, VM),
        out_shape=(jax.ShapeDtypeStruct((ROWS, C), bf16), jax.ShapeDtypeStruct((ROWS, D), f32)),
        scratch_shapes=[pltpu.VMEM((C // 128, 4 * ROWS, 128), f32)] * 2,
        name="conv",
    )(scal, frames, conv1_weight, row(conv1_gain), conv2_weight, row(conv2_gain), row(proj_gain), proj_weight,
      row(mask_embed), *spans)

    up, down = [normed], [normed]
    for _ in range(3):
        up.append(lax.ppermute(up[-1], "tm", z_perm(-1)))
        down.append(lax.ppermute(down[-1], "tm", z_perm(1)))
    half = ROWS // 2
    far = [lax.ppermute(down[3][:half], "tm", z_perm(1)), lax.ppermute(up[3][half:], "tm", z_perm(-1))]
    rows_all = jnp.concatenate(up[:4] + far + [down[3], down[2], down[1]])

    block = 2 * ROWS
    queries, kv = pl.pallas_call(
        qkv_kernel,
        grid=(GROUP // block,),
        in_specs=[SM, SM, pl.BlockSpec((block, C), lambda i: (i, 0))] + [VM] * 6,
        out_specs=(pl.BlockSpec((block, 512), lambda i: (i, 0)), pl.BlockSpec((2 * PAIR, block), lambda i: (0, i))),
        out_shape=(jax.ShapeDtypeStruct((GROUP, 512), bf16), jax.ShapeDtypeStruct((2 * PAIR, GROUP), bf16)),
        scratch_shapes=[pltpu.VMEM((D, 3 * PAIR), bf16)],
        name="qkv",
    )(scal, idx, rows_all, proj_weight, row(mask_embed), row(attn_gain), *spans, w_blocks)

    ahead = lax.ppermute(kv, "tm", y_perm(-1))
    behind = lax.ppermute(kv, "tm", y_perm(1))
    across = jnp.concatenate([
        lax.ppermute(ahead[:PAIR], "tm", y_perm(-1)),
        lax.ppermute(behind[PAIR:], "tm", y_perm(1)),
    ])
    o_blocks = share([out_weight] * NY)
    state = attend((0,), True, False, scal, queries, (kv,), None)
    state = attend((1, 3), False, False, scal, queries, (ahead, behind), state)
    packed = attend((2,), False, True, scal, queries, (across,), state)
    back = [packed[0]] + [lax.ppermute(packed[j], "tm", z_perm(j)) for j in range(1, NZ)]
    return pl.pallas_call(
        out_kernel,
        in_specs=[SM, SM] + [VM] * 3,
        out_specs=VM,
        out_shape=jax.ShapeDtypeStruct((ROWS, D), bf16),
        scratch_shapes=[pltpu.VMEM((D, D), bf16)],
        name="out",
    )(scal, idx, residual, jnp.stack(back), o_blocks)


def solution(mesh):
    return jax.shard_map(
        local,
        mesh=mesh,
        in_specs=(
            P(("seg", "tm"), None), P(), P(), P(), P(), P(), P(), P(), P(),
            P("tm", None), P("tm", None), P("seg"), P("seg"), P("seg"),
        ),
        out_specs=P(("seg", "tm"), None),
        check_vma=False,
    )
```

```python
import functools

import jax
import jax.numpy as jnp
from jax import lax
from jax.experimental import pallas as pl
from jax.experimental.pallas import tpu as pltpu
from jax.sharding import PartitionSpec as P

HEADS = 16
NY, NZ = 4, 8
ROWS = 192
GROUP = ROWS * NZ
C = 512
D = 1280
HD = 80
PAIR = 2 * HD
EPS = 1e-05
LOG2E = 1.4426950408889634
LOW = -1e30
f32, bf16 = jnp.float32, jnp.bfloat16
VM = pl.BlockSpec(memory_space=pltpu.VMEM)
SM = pl.BlockSpec(memory_space=pltpu.SMEM)


def norm(values, gain_row):
    center = values - jnp.mean(values, axis=-1, keepdims=True)
    spread = jnp.mean(center * center, axis=-1, keepdims=True)
    return center * lax.rsqrt(spread + EPS) * gain_row


def gelu(v):
    return 0.5 * v * (1.0 + lax.erf(v * 0.7071067811865476))


def mm(a, b):
    return jnp.dot(a, b, preferred_element_type=f32)


def row(ref):
    return ref[...].reshape(1, -1)


def residual_of(normed, proj_weight, embed, starts, lengths, position, valid):
    projected = mm(normed, proj_weight)
    hit = (position >= starts) & (position < starts + lengths)
    covered = jnp.max(hit.astype(jnp.int32), axis=1, keepdims=True) > 0
    residual = jnp.where(covered, embed, projected)
    return jnp.where(position < valid, residual, 0.0)


def place():
    t = lax.axis_index("tm")
    return t // NZ, t & (NZ - 1)


def pick_kernel(w_ref, out_ref):
    target = (place()[1] - lax.axis_index("seg")) & (NZ - 1)
    for i in range(NZ):
        @pl.when(target == i)
        def _(i=i):
            out_ref[...] = jnp.concatenate(
                [w_ref[:, D * j + PAIR * i:D * j + PAIR * i + PAIR] for j in range(3)], axis=1)


def pack_kernel(*refs):
    y = place()[0]
    for k in range(NY):
        refs[NY][(y + k) & (NY - 1)] = refs[k][...]


def spread(parts, hold, out_ref):
    z = place()[1]
    s = lax.axis_index("seg")
    for cross in range(2):
        for dx in range(4):
            source = (((s // 2 + dx) & 3) * 2 + ((s + cross) & 1) + z) & (NZ - 1)
            hold[source] = parts[cross * 4 + dx][...]
    for i in range(NY * NZ):
        out_ref[40 * i:40 * i + 40, :] = hold[i % NZ, i // NZ]


def spread_kernel(*refs):
    spread(refs[:8], refs[9], refs[8])


def conv_kernel(valid_ref, x_ref, w1_ref, g1_ref, w2_ref, g2_ref, pg_ref, pw_ref, me_ref, st_ref, ln_ref,
                normed_ref, res_ref, a_ref, b_ref):
    def pairs(inputs, w_ref, rows):
        left = mm(inputs, w_ref[:C, :])
        right = mm(inputs, w_ref[C:, :])
        parts = []
        for i in range(C // 128):
            a_ref[i, pl.ds(0, 2 * rows), :] = left[:, 128 * i:128 * i + 128]
            b_ref[i, pl.ds(0, 2 * rows), :] = right[:, 128 * i:128 * i + 128]
            parts.append(a_ref[i, pl.ds(0, rows, stride=2), :] + b_ref[i, pl.ds(1, rows, stride=2), :])
        return jnp.concatenate(parts, axis=1)

    first = gelu(norm(pairs(x_ref[...], w1_ref, 2 * ROWS), row(g1_ref))).astype(bf16)
    second = gelu(norm(pairs(first, w2_ref, ROWS), row(g2_ref))).astype(bf16)
    normed = norm(second.astype(f32), row(pg_ref)).astype(bf16)
    normed_ref[...] = normed
    position = lax.axis_index("tm") * ROWS + lax.broadcasted_iota(jnp.int32, (ROWS, 1), 0)
    res_ref[...] = residual_of(normed, pw_ref[...], row(me_ref), row(st_ref), row(ln_ref), position, valid_ref[0])


SLOTS = ((1, 7, 2, 6), (3, 5, 0, 4))


def qkv_kernel(half, count, valid_ref, pw_ref, me_ref, ag_ref, st_ref, ln_ref, *refs):
    blocks = refs[:count]
    rest = refs[count:]
    if half == 0:
        parts, (q_ref, kv_ref, ws_ref, hold) = rest[:8], rest[8:]
        spread(parts, hold, ws_ref)
    else:
        ws_ref, _, q_ref, kv_ref = rest
    block = 2 * ROWS
    y, z = place()
    rows_in = lax.broadcasted_iota(jnp.int32, (block, 1), 0)
    for p in range(2):
        ends = [((z + SLOTS[half][2 * p + i]) & (NZ - 1)) * ROWS for i in range(2)]
        position = y * GROUP + rows_in + jnp.where(rows_in < ROWS, ends[0], ends[1] - ROWS)
        inputs = jnp.concatenate([b[...] for b in blocks[2 * p:count if p else 2]], axis=0)
        residual = residual_of(inputs, pw_ref[...], row(me_ref), row(st_ref), row(ln_ref), position, valid_ref[0])
        attn_in = norm(residual, row(ag_ref)).astype(bf16)
        joined = mm(attn_in, ws_ref[...]).astype(bf16)
        scaled = joined[:, :PAIR].astype(f32) * (LOG2E * HD ** -0.5)
        hi = scaled.astype(bf16)
        lo = (scaled - hi.astype(f32)).astype(bf16)
        one = jnp.ones((block, 1), bf16)
        pad = jnp.zeros((block, 95), bf16)
        parts = []
        for h in range(2):
            parts += [hi[:, h * HD:h * HD + HD], lo[:, h * HD:h * HD + HD], one, pad]
        q_ref[block * p:block * p + block, :] = jnp.concatenate(parts, axis=1)
        kv_ref[:, block * p:block * p + block] = joined[:, PAIR:].astype(f32).T.astype(bf16)


def attend_kernel(offsets, first, last, *refs):
    count = len(offsets)
    valid_ref, q_ref = refs[:2]
    kv_refs = refs[2:2 + 2 * count]
    rest = refs[2 + 2 * count:]
    if first:
        out_ref, kk, vv = rest
        prev = None
    else:
        prev, out_ref, kk, vv = rest
    block = 2 * ROWS
    half = GROUP // 2
    valid = valid_ref[0]
    y, z = place()
    base = [((y + d) & (NY - 1)) * GROUP for d in offsets]

    @pl.when(pl.program_id(0) == 0)
    def _():
        lane = lax.broadcasted_iota(jnp.int32, (16, half), 1)
        line = lax.broadcasted_iota(jnp.int32, (16, half), 0)
        for c in range(count):
            for p in range(2):
                cols = pl.ds(half * p, half)
                spot = lane
                for i in range(4):
                    shift = ((z + SLOTS[p][i]) & (NZ - 1)) * ROWS - i * ROWS
                    spot = jnp.where(lane // ROWS == i, lane + shift, spot)
                bias = jnp.where((line == 0) & (base[c] + spot >= valid), LOW, 0.0).astype(bf16)
                kv = kv_refs[2 * c + p]
                for h in range(2):
                    keys = kv[h * HD:h * HD + HD, :]
                    kk[c, h, 0:HD, cols] = keys
                    kk[c, h, HD:2 * HD, cols] = keys
                    kk[c, h, 2 * HD:2 * HD + 16, cols] = bias
                    kk[c, h, 2 * HD + 16:, cols] = jnp.zeros((80, half), bf16)
                    vv[c, h, 0:HD, cols] = kv[PAIR + h * HD:PAIR + h * HD + HD, :]
                    vv[c, h, HD:HD + 16, cols] = jnp.where(line == 0, 1.0, 0.0).astype(bf16)
                    vv[c, h, HD + 16:, cols] = jnp.zeros((32, half), bf16)

    lane = lax.broadcasted_iota(jnp.int32, (block, 128), 1)
    if first:
        state = [jnp.where(lane == HD + 1, LOW, 0.0)] * 2
    else:
        state = [prev[:, h * 128:h * 128 + 128] for h in range(2)]

    def chunk_step(c, state):
        new = []
        for h in range(2):
            scores = mm(q_ref[:, h * 256:h * 256 + 256], kk[c, h])
            old = state[h][:, HD + 1:HD + 2]
            peak = jnp.maximum(old, jnp.max(scores, axis=1, keepdims=True))
            weights = jnp.exp2(scores - peak).astype(bf16)
            mixed = lax.dot_general(weights, vv[c, h], (((1,), (1,)), ((), ())), preferred_element_type=f32)
            acc = state[h] * jnp.exp2(old - peak) + mixed
            new.append(jnp.where(lane == HD + 1, peak, acc))
        return new

    for c in range(count):
        state = lax.cond(base[c] < valid, functools.partial(chunk_step, c), lambda s: s, state)
    if last:
        done = [(state[h] / state[h][:, HD:HD + 1])[:, :HD] for h in range(2)]
        both = jnp.concatenate(done, axis=1)
        for b in range(2):
            rows = both[b * ROWS:b * ROWS + ROWS]
            out_ref[b, 0:ROWS, :] = rows[:, :128].astype(bf16)
            tail = rows[:, 128:]
            packed = jnp.concatenate([tail[48 * i:48 * i + 48] for i in range(4)], axis=1)
            out_ref[b, ROWS:, :] = packed.astype(bf16)
    else:
        for h in range(2):
            out_ref[:, h * 128:h * 128 + 128] = state[h]


def attend(offsets, first, last, valid, queries, chunks, state):
    count = len(offsets)
    block = 2 * ROWS
    kv_spec = pl.BlockSpec((2 * PAIR, GROUP // 2), lambda i: (0, 0))
    state_spec = pl.BlockSpec((block, 256), lambda i: (i, 0))
    in_specs = [SM, pl.BlockSpec((block, 512), lambda i: (i, 0))] + [kv_spec] * (2 * count)
    args = [valid, queries] + list(chunks)
    if not first:
        in_specs.append(state_spec)
        args.append(state)
    if last:
        out_shape = jax.ShapeDtypeStruct((NZ, 240, 128), bf16)
        out_spec = pl.BlockSpec((2, 240, 128), lambda i: (i, 0, 0))
    else:
        out_shape = jax.ShapeDtypeStruct((GROUP, 256), f32)
        out_spec = state_spec
    return pl.pallas_call(
        functools.partial(attend_kernel, offsets, first, last),
        grid=(GROUP // block,),
        in_specs=in_specs,
        out_specs=out_spec,
        out_shape=out_shape,
        scratch_shapes=[pltpu.VMEM((count, 2, 256, GROUP), bf16), pltpu.VMEM((count, 2, 128, GROUP), bf16)],
        cost_estimate=pl.CostEstimate(
            flops=count * 4 * GROUP * GROUP * 512, bytes_accessed=count * 2 * PAIR * GROUP * 2,
            transcendentals=count * 2 * GROUP * GROUP),
        name="attend_%d_%d" % (count, int(last)),
    )(*args)


def out_kernel(valid_ref, res_ref, *refs):
    m_refs, os_ref, out_ref = refs[:NZ], refs[NZ], refs[NZ + 1]
    z = place()[1]
    total = res_ref[...]
    for j in range(NZ):
        m_ref = m_refs[j]
        tail = m_ref[ROWS:, :]
        tail = jnp.concatenate([tail[:, 32 * i:32 * i + 32] for i in range(4)], axis=0)
        merged = jnp.concatenate([m_ref[:ROWS, :], tail], axis=1)
        start = pl.multiple_of(((z - j) & (NZ - 1)) * PAIR, PAIR)
        total = total + mm(merged, os_ref[pl.ds(start, PAIR), :])
    position = lax.axis_index("tm") * ROWS + lax.broadcasted_iota(jnp.int32, (ROWS, 1), 0)
    out_ref[...] = jnp.where(position < valid_ref[0], total, 0.0).astype(bf16)


def z_perm(shift):
    return [(y * NZ + z, y * NZ + (z + shift) % NZ) for y in range(NY) for z in range(NZ)]


def y_perm(shift):
    return [(y * NZ + z, ((y + shift) % NY) * NZ + z) for y in range(NY) for z in range(NZ)]


def seg_perm(shift):
    return [(s, (s + shift) % 8) for s in range(8)]


def fetch_perm():
    return [
        (s * 32 + y * NZ + (z + s) % NZ, s * 32 + y * NZ + z)
        for s in range(8) for y in range(NY) for z in range(NZ)
    ]


def share(block):
    near = [block] + [lax.ppermute(block, "tm", y_perm(-k)) for k in range(1, NY)]
    packed = pl.pallas_call(
        pack_kernel, in_specs=[VM] * NY, out_specs=VM,
        out_shape=jax.ShapeDtypeStruct((NY,) + block.shape, block.dtype), name="pack",
    )(*near)
    got = lax.ppermute(packed, ("seg", "tm"), fetch_perm())
    mine = [got] + [lax.ppermute(got, "seg", seg_perm(-2 * d)) for d in range(1, 4)]
    return mine + [lax.ppermute(m, "seg", [(s, s ^ 1) for s in range(8)]) for m in mine]


def local(frames, conv1_weight, conv1_gain, conv2_weight, conv2_gain, proj_gain, proj_weight, mask_embed,
          attn_gain, qkv_weight, out_weight, span_starts, span_lengths, valid_count):
    columns = pl.pallas_call(
        pick_kernel, in_specs=[VM], out_specs=VM,
        out_shape=jax.ShapeDtypeStruct((40, 3 * PAIR), bf16), name="pick",
    )(qkv_weight)
    w_parts = share(columns)

    normed, residual = pl.pallas_call(
        conv_kernel,
        in_specs=[SM] + [VM] * 10,
        out_specs=(VM, VM),
        out_shape=(jax.ShapeDtypeStruct((ROWS, C), bf16), jax.ShapeDtypeStruct((ROWS, D), f32)),
        scratch_shapes=[pltpu.VMEM((C // 128, 4 * ROWS, 128), f32)] * 2,
        cost_estimate=pl.CostEstimate(flops=4 * 10**9, bytes_accessed=6 * 10**6, transcendentals=0),
        name="conv",
    )(valid_count, frames, conv1_weight, conv1_gain, conv2_weight, conv2_gain, proj_gain, proj_weight,
      mask_embed, span_starts, span_lengths)

    up, down = [normed], [normed]
    for _ in range(3):
        up.append(lax.ppermute(up[-1], "tm", z_perm(-1)))
        down.append(lax.ppermute(down[-1], "tm", z_perm(1)))
    half = ROWS // 2
    far = [lax.ppermute(down[3][:half], "tm", z_perm(1)), lax.ppermute(up[3][half:], "tm", z_perm(-1))]

    shared = (valid_count, proj_weight, mask_embed, attn_gain, span_starts, span_lengths)
    q_shape = jax.ShapeDtypeStruct((GROUP, 512), bf16)
    kv_shape = jax.ShapeDtypeStruct((2 * PAIR, GROUP // 2), bf16)
    w_shape = jax.ShapeDtypeStruct((D, 3 * PAIR), bf16)
    q_spec = [pl.BlockSpec((GROUP // 2, 512), functools.partial(lambda h, i: (h, 0), h)) for h in range(2)]
    cost = pl.CostEstimate(flops=8 * 10**9, bytes_accessed=4 * 10**6, transcendentals=0)
    queries, kv_a, w_all = pl.pallas_call(
        functools.partial(qkv_kernel, 0, 4),
        grid=(1,),
        in_specs=[SM] + [VM] * 17,
        out_specs=(q_spec[0], VM, VM),
        out_shape=(q_shape, kv_shape, w_shape),
        scratch_shapes=[pltpu.VMEM((NZ, NY, 40, 3 * PAIR), bf16)],
        cost_estimate=cost,
        name="qkv0",
    )(*shared, up[1], down[1], up[2], down[2], *w_parts)
    queries, kv_b = pl.pallas_call(
        functools.partial(qkv_kernel, 1, 5),
        grid=(1,),
        in_specs=[SM] + [VM] * 11 + [pl.BlockSpec(memory_space=pl.ANY)],
        out_specs=(q_spec[1], VM),
        out_shape=(q_shape, kv_shape),
        input_output_aliases={12: 0},
        cost_estimate=cost,
        name="qkv1",
    )(*shared, up[3], down[3], normed, *far, w_all, queries)

    ahead = [lax.ppermute(kv, "tm", y_perm(-1)) for kv in (kv_a, kv_b)]
    behind = [lax.ppermute(kv, "tm", y_perm(1)) for kv in (kv_a, kv_b)]
    across = [lax.ppermute(ahead[0], "tm", y_perm(-1)), lax.ppermute(behind[1], "tm", y_perm(1))]
    o_parts = share(lax.optimization_barrier((out_weight, kv_b))[0])
    state = attend((0,), True, False, valid_count, queries, (kv_a, kv_b), None)
    state = attend((1, 3), False, False, valid_count, queries, ahead + behind, state)
    packed = attend((2,), False, True, valid_count, queries, across, state)
    *o_parts, packed = lax.optimization_barrier((*o_parts, packed))
    o_all = pl.pallas_call(
        spread_kernel, in_specs=[VM] * 8, out_specs=VM,
        out_shape=jax.ShapeDtypeStruct((D, D), bf16),
        scratch_shapes=[pltpu.VMEM((NZ, NY, 40, D), bf16)],
        name="spread",
    )(*o_parts)
    order = SLOTS[0] + SLOTS[1]
    back = [lax.ppermute(packed[order.index(j)], "tm", z_perm(j)) if j else packed[order.index(0)] for j in range(NZ)]
    return pl.pallas_call(
        out_kernel,
        in_specs=[SM] + [VM] * 10,
        out_specs=VM,
        out_shape=jax.ShapeDtypeStruct((ROWS, D), bf16),
        name="out",
    )(valid_count, residual, *back, o_all)


def solution(mesh):
    return jax.shard_map(
        local,
        mesh=mesh,
        in_specs=(
            P(("seg", "tm"), None), P(), P(), P(), P(), P(), P(), P(), P(),
            P("tm", None), P("tm", None), P("seg"), P("seg"), P("seg"),
        ),
        out_specs=P(("seg", "tm"), None),
        check_vma=False,
    )
```

```python
import functools

import jax
import jax.numpy as jnp
from jax import lax
from jax.experimental import pallas as pl
from jax.experimental.pallas import tpu as pltpu
from jax.sharding import PartitionSpec as P


NY, NZ = 4, 8
ROWS = 192
GROUP = ROWS * NZ
C = 512
D = 1280
HD = 80
PAIR = 2 * HD
EPS = 1e-05
LOG2E = 1.4426950408889634
LOW = -1e30
BLOCK, KEYS = 768, 512
f32, bf16 = jnp.float32, jnp.bfloat16
VM = pl.BlockSpec(memory_space=pltpu.VMEM)
SM = pl.BlockSpec(memory_space=pltpu.SMEM)


def norm(values, gain_row):
    center = values - jnp.mean(values, axis=-1, keepdims=True)
    spread = jnp.mean(center * center, axis=-1, keepdims=True)
    return center * lax.rsqrt(spread + EPS) * gain_row


def gelu(v):
    return 0.5 * v * (1.0 + lax.erf(v * 0.7071067811865476))


def mm(a, b):
    return jnp.dot(a, b, preferred_element_type=f32)


def row(ref):
    return ref[...].reshape(1, -1)


def residual_of(normed, proj_weight, embed, starts, lengths, position, valid):
    projected = mm(normed, proj_weight)
    hit = (position >= starts) & (position < starts + lengths)
    covered = jnp.max(hit.astype(jnp.int32), axis=1, keepdims=True) > 0
    residual = jnp.where(covered, embed, projected)
    return jnp.where(position < valid, residual, 0.0)


def place():
    t = lax.axis_index("tm")
    return t // NZ, t & (NZ - 1)


def shift_of(x, c):
    return jnp.where(c == 0, x, jnp.where(x == 0, 4, NZ - x))


def pick_kernel(w_ref, ow_ref, out_ref):
    s = lax.axis_index("seg")
    target = (place()[1] - shift_of(s // 2, s & 1)) & (NZ - 1)
    out_ref[:, :D] = ow_ref[...]
    for i in range(NZ):
        @pl.when(target == i)
        def _(i=i):
            out_ref[:, D:] = jnp.concatenate(
                [w_ref[:, D * j + PAIR * i:D * j + PAIR * i + PAIR] for j in range(3)], axis=1)


def pack_kernel(*refs):
    y = place()[0]
    for k in range(NY):
        refs[NY][(y + k) & (NY - 1)] = refs[k][:, D:]
        refs[NY + 1][(y + k) & (NY - 1)] = refs[k][:, :D]


def spread(parts, hold, out_ref):
    z = place()[1]
    s = lax.axis_index("seg")
    for cross in range(2):
        for dx in range(4):
            source = (shift_of((s // 2 + dx) & 3, (s + cross) & 1) + z) & (NZ - 1)
            hold[source] = parts[cross * 4 + dx][...]
    for i in range(NY * NZ):
        out_ref[40 * i:40 * i + 40, :] = hold[i % NZ, i // NZ]


def spread_kernel(*refs):
    spread(refs[:8], refs[9], refs[8])


def conv_kernel(valid_ref, x_ref, w1_ref, g1_ref, w2_ref, g2_ref, pg_ref, pw_ref, me_ref, st_ref, ln_ref,
                normed_ref, res_ref, a_ref, b_ref):
    def pairs(inputs, w_ref, rows):
        left = mm(inputs, w_ref[:C, :])
        right = mm(inputs, w_ref[C:, :])
        parts = []
        for i in range(C // 128):
            a_ref[i, pl.ds(0, 2 * rows), :] = left[:, 128 * i:128 * i + 128]
            b_ref[i, pl.ds(0, 2 * rows), :] = right[:, 128 * i:128 * i + 128]
            parts.append(a_ref[i, pl.ds(0, rows, stride=2), :] + b_ref[i, pl.ds(1, rows, stride=2), :])
        return jnp.concatenate(parts, axis=1)

    first = gelu(norm(pairs(x_ref[...], w1_ref, 2 * ROWS), row(g1_ref))).astype(bf16)
    second = gelu(norm(pairs(first, w2_ref, ROWS), row(g2_ref))).astype(bf16)
    normed = norm(second.astype(f32), row(pg_ref)).astype(bf16)
    normed_ref[...] = normed
    position = lax.axis_index("tm") * ROWS + lax.broadcasted_iota(jnp.int32, (ROWS, 1), 0)
    res_ref[...] = residual_of(normed, pw_ref[...], row(me_ref), row(st_ref), row(ln_ref), position, valid_ref[0])


SLOTS = ((1, 7, 2, 6), (3, 5, 0, 4))


def qkv_kernel(half, count, valid_ref, pw_ref, me_ref, ag_ref, st_ref, ln_ref, *refs):
    blocks = refs[:count]
    rest = refs[count:]
    if half == 0:
        parts, (q_ref, kv_ref, ws_ref, hold) = rest[:8], rest[8:]
        spread(parts, hold, ws_ref)
    else:
        ws_ref, _, q_ref, kv_ref = rest
    block = 2 * ROWS
    y, z = place()
    rows_in = lax.broadcasted_iota(jnp.int32, (block, 1), 0)
    for p in range(2):
        ends = [((z + SLOTS[half][2 * p + i]) & (NZ - 1)) * ROWS for i in range(2)]
        position = y * GROUP + rows_in + jnp.where(rows_in < ROWS, ends[0], ends[1] - ROWS)
        inputs = jnp.concatenate([b[...] for b in blocks[2 * p:count if p else 2]], axis=0)
        residual = residual_of(inputs, pw_ref[...], row(me_ref), row(st_ref), row(ln_ref), position, valid_ref[0])
        attn_in = norm(residual, row(ag_ref)).astype(bf16)
        joined = mm(attn_in, ws_ref[...]).astype(bf16)
        scaled = joined[:, :PAIR].astype(f32) * (LOG2E * HD ** -0.5)
        hi = scaled.astype(bf16)
        lo = (scaled - hi.astype(f32)).astype(bf16)
        one = jnp.ones((block, 1), bf16)
        pad = jnp.zeros((block, 95), bf16)
        parts = []
        for h in range(2):
            parts += [hi[:, h * HD:h * HD + HD], lo[:, h * HD:h * HD + HD], one, pad]
        q_ref[block * p:block * p + block, :] = jnp.concatenate(parts, axis=1)
        kv_ref[:, block * p:block * p + block] = joined[:, PAIR:].astype(f32).T.astype(bf16)


def attend_kernel(offsets, first, last, *refs):
    count = len(offsets)
    valid_ref, q_ref = refs[:2]
    kv_refs = refs[2:2 + 2 * count]
    rest = refs[2 + 2 * count:]
    prev = None if first else rest[0]
    outs = rest[int(not first):-3]
    kk, vv, acc = rest[-3:]
    block = BLOCK
    half = GROUP // 2
    valid = valid_ref[0]
    y, z = place()
    base = [((y + d) & (NY - 1)) * GROUP for d in offsets]

    @pl.when(pl.program_id(0) == 0)
    def _():
        lane = lax.broadcasted_iota(jnp.int32, (16, half), 1)
        line = lax.broadcasted_iota(jnp.int32, (16, half), 0)
        for c in range(count):
            for p in range(2):
                cols = pl.ds(half * p, half)
                spot = lane
                for i in range(4):
                    shift = ((z + SLOTS[p][i]) & (NZ - 1)) * ROWS - i * ROWS
                    spot = jnp.where(lane // ROWS == i, lane + shift, spot)
                bias = jnp.where((line == 0) & (base[c] + spot >= valid), LOW, 0.0).astype(bf16)
                kv = kv_refs[2 * c + p]
                for h in range(2):
                    keys = kv[h * HD:h * HD + HD, :]
                    kk[c, h, 0:HD, cols] = keys
                    kk[c, h, HD:2 * HD, cols] = keys
                    kk[c, h, 2 * HD:2 * HD + 16, cols] = bias
                    kk[c, h, 2 * HD + 16:, cols] = jnp.zeros((80, half), bf16)
                    vv[c, h, 0:HD, cols] = kv[PAIR + h * HD:PAIR + h * HD + HD, :]
                    vv[c, h, HD:HD + 16, cols] = jnp.where(line == 0, 1.0, 0.0).astype(bf16)
                    vv[c, h, HD + 16:, cols] = jnp.zeros((32, half), bf16)

    lane = lax.broadcasted_iota(jnp.int32, (block, 128), 1)
    for h in range(2):
        acc[h] = jnp.where(lane == HD + 1, LOW, 0.0) if first else prev[:, h * 128:h * 128 + 128]

    def chunk_step(c, carry):
        @pl.when(((y + pick(offsets, c)) & (NY - 1)) * GROUP < valid)
        def _():
            for h in range(2):
                state = acc[h]
                old = state[:, HD + 1:HD + 2]
                for k in range(GROUP // KEYS):
                    cols = slice(k * KEYS, k * KEYS + KEYS)
                    scores = mm(q_ref[:, h * 256:h * 256 + 256], kk[c, h, :, cols])
                    peak = jnp.maximum(old, jnp.max(scores, axis=1, keepdims=True))
                    weights = jnp.exp2(scores - peak).astype(bf16)
                    mixed = lax.dot_general(
                        weights, vv[c, h, :, cols], (((1,), (1,)), ((), ())), preferred_element_type=f32)
                    state = state * jnp.exp2(old - peak) + mixed
                    old = peak
                acc[h] = jnp.where(lane == HD + 1, old, state)

        return carry

    lax.fori_loop(0, count, chunk_step, 0)
    if last:
        both = jnp.concatenate([(acc[h] / acc[h][:, HD:HD + 1])[:, :HD] for h in range(2)], axis=1)
        for b in range(block // ROWS):
            rows = both[b * ROWS:b * ROWS + ROWS]
            tail = rows[:, 128:]
            packed = jnp.concatenate([tail[48 * i:48 * i + 48] for i in range(4)], axis=1)
            for g in range(GROUP // block):
                @pl.when(pl.program_id(0) == g)
                def _(b=b, g=g, rows=rows, packed=packed):
                    outs[g * (block // ROWS) + b][0:ROWS, :] = rows[:, :128].astype(bf16)
                    outs[g * (block // ROWS) + b][ROWS:, :] = packed.astype(bf16)
    else:
        for h in range(2):
            outs[0][:, h * 128:h * 128 + 128] = acc[h]


def pick(values, index):
    got = jnp.int32(values[0])
    for i, v in enumerate(values[1:]):
        got = jnp.where(index == i + 1, v, got)
    return got


def attend(offsets, first, last, valid, queries, chunks, state):
    count = len(offsets)
    block = BLOCK
    kv_spec = pl.BlockSpec((2 * PAIR, GROUP // 2), lambda i: (0, 0))
    state_spec = pl.BlockSpec((block, 256), lambda i: (i, 0))
    in_specs = [SM, pl.BlockSpec((block, 512), lambda i: (i, 0))] + [kv_spec] * (2 * count)
    args = [valid, queries] + list(chunks)
    if not first:
        in_specs.append(state_spec)
        args.append(state)
    if last:
        out_shape = [jax.ShapeDtypeStruct((240, 128), bf16)] * NZ
        out_spec = [pl.BlockSpec((240, 128), lambda i: (0, 0))] * NZ
    else:
        out_shape = jax.ShapeDtypeStruct((GROUP, 256), f32)
        out_spec = state_spec
    return pl.pallas_call(
        functools.partial(attend_kernel, offsets, first, last),
        grid=(GROUP // block,),
        in_specs=in_specs,
        out_specs=out_spec,
        out_shape=out_shape,
        scratch_shapes=[pltpu.VMEM((count, 2, 256, GROUP), bf16), pltpu.VMEM((count, 2, 128, GROUP), bf16),
                        pltpu.VMEM((2, block, 128), f32)],
        cost_estimate=pl.CostEstimate(
            flops=count * 4 * GROUP * GROUP * 512, bytes_accessed=count * 2 * PAIR * GROUP * 2,
            transcendentals=count * 2 * GROUP * GROUP),
    )(*args)


def out_kernel(valid_ref, res_ref, *refs):
    m_refs, os_ref, out_ref = refs[:NZ], refs[NZ], refs[NZ + 1]
    z = place()[1]
    total = res_ref[...]
    for j in range(NZ):
        m_ref = m_refs[j]
        tail = m_ref[ROWS:, :]
        tail = jnp.concatenate([tail[:, 32 * i:32 * i + 32] for i in range(4)], axis=0)
        merged = jnp.concatenate([m_ref[:ROWS, :], tail], axis=1)
        start = pl.multiple_of(((z - j) & (NZ - 1)) * PAIR, PAIR)
        total = total + mm(merged, os_ref[pl.ds(start, PAIR), :])
    position = lax.axis_index("tm") * ROWS + lax.broadcasted_iota(jnp.int32, (ROWS, 1), 0)
    out_ref[...] = jnp.where(position < valid_ref[0], total, 0.0).astype(bf16)


def z_perm(shift):
    return [(y * NZ + z, y * NZ + (z + shift) % NZ) for y in range(NY) for z in range(NZ)]


def y_perm(shift):
    return [(y * NZ + z, ((y + shift) % NY) * NZ + z) for y in range(NY) for z in range(NZ)]


def seg_perm(shift):
    return [(s, (s + shift) % 8) for s in range(8)]


def fetch_perm():
    shift = lambda s: s // 2 if s % 2 == 0 else (NZ - s // 2 if s > 1 else 4)
    return [
        (s * 32 + y * NZ + (z + shift(s)) % NZ, s * 32 + y * NZ + z)
        for s in range(8) for y in range(NY) for z in range(NZ)
    ]


def share(got):
    mine = [got] + [lax.ppermute(got, "seg", seg_perm(-2 * d)) for d in range(1, 4)]
    return mine + [lax.ppermute(m, "seg", [(s, s ^ 1) for s in range(8)]) for m in mine]


def encode(frames, conv1_weight, conv1_gain, conv2_weight, conv2_gain, proj_gain, proj_weight, mask_embed,
           attn_gain, qkv_weight, out_weight, span_starts, span_lengths, valid_count):
    columns = pl.pallas_call(
        pick_kernel, in_specs=[VM, VM], out_specs=VM,
        out_shape=jax.ShapeDtypeStruct((40, D + 3 * PAIR), bf16), name="pick",
    )(qkv_weight, out_weight)
    fetched = lax.ppermute(columns, ("seg", "tm"), fetch_perm())
    near = [fetched] + [lax.ppermute(fetched, "tm", y_perm(-k)) for k in range(1, NY)]
    w_pack, o_pack = pl.pallas_call(
        pack_kernel, in_specs=[VM] * NY, out_specs=(VM, VM),
        out_shape=(jax.ShapeDtypeStruct((NY, 40, 3 * PAIR), bf16), jax.ShapeDtypeStruct((NY, 40, D), bf16)),
        name="pack",
    )(*near)
    w_parts = share(w_pack)

    normed, residual = pl.pallas_call(
        conv_kernel,
        in_specs=[SM] + [VM] * 10,
        out_specs=(VM, VM),
        out_shape=(jax.ShapeDtypeStruct((ROWS, C), bf16), jax.ShapeDtypeStruct((ROWS, D), f32)),
        scratch_shapes=[pltpu.VMEM((C // 128, 4 * ROWS, 128), f32)] * 2,
        cost_estimate=pl.CostEstimate(flops=4 * 10**9, bytes_accessed=6 * 10**6, transcendentals=0),
        name="conv",
    )(valid_count, frames, conv1_weight, conv1_gain, conv2_weight, conv2_gain, proj_gain, proj_weight,
      mask_embed, span_starts, span_lengths)

    up, down = [normed], [normed]
    for _ in range(3):
        up.append(lax.ppermute(up[-1], "tm", z_perm(-1)))
        down.append(lax.ppermute(down[-1], "tm", z_perm(1)))
    half = ROWS // 2
    far = [lax.ppermute(down[3][:half], "tm", z_perm(1)), lax.ppermute(up[3][half:], "tm", z_perm(-1))]

    shared = (valid_count, proj_weight, mask_embed, attn_gain, span_starts, span_lengths)
    q_shape = jax.ShapeDtypeStruct((GROUP, 512), bf16)
    kv_shape = jax.ShapeDtypeStruct((2 * PAIR, GROUP // 2), bf16)
    w_shape = jax.ShapeDtypeStruct((D, 3 * PAIR), bf16)
    q_spec = [pl.BlockSpec((GROUP // 2, 512), functools.partial(lambda h, i: (h, 0), h)) for h in range(2)]
    cost = pl.CostEstimate(flops=8 * 10**9, bytes_accessed=4 * 10**6, transcendentals=0)
    queries, kv_a, w_all = pl.pallas_call(
        functools.partial(qkv_kernel, 0, 4),
        grid=(1,),
        in_specs=[SM] + [VM] * 17,
        out_specs=(q_spec[0], VM, VM),
        out_shape=(q_shape, kv_shape, w_shape),
        scratch_shapes=[pltpu.VMEM((NZ, NY, 40, 3 * PAIR), bf16)],
        cost_estimate=cost,
        name="qkv0",
    )(*shared, up[1], down[1], up[2], down[2], *w_parts)
    queries, kv_b = pl.pallas_call(
        functools.partial(qkv_kernel, 1, 5),
        grid=(1,),
        in_specs=[SM] + [VM] * 11 + [pl.BlockSpec(memory_space=pl.ANY)],
        out_specs=(q_spec[1], VM),
        out_shape=(q_shape, kv_shape),
        input_output_aliases={12: 0},
        cost_estimate=cost,
        name="qkv1",
    )(*shared, up[3], down[3], normed, *far, w_all, queries)

    ahead = [lax.ppermute(kv, "tm", y_perm(-1)) for kv in (kv_a, kv_b)]
    behind = [lax.ppermute(kv, "tm", y_perm(1)) for kv in (kv_a, kv_b)]
    across = [lax.ppermute(ahead[0], "tm", y_perm(-1)), lax.ppermute(behind[1], "tm", y_perm(1))]
    o_parts = share(lax.optimization_barrier((o_pack, kv_b))[0])
    state = attend((0,), True, False, valid_count, queries, (kv_a, kv_b), None)
    state = attend((1, 3), False, False, valid_count, queries, ahead + behind, state)
    packed = list(attend((2,), False, True, valid_count, queries, across, state))
    *o_parts, packed[0] = lax.optimization_barrier((*o_parts, packed[0]))
    o_all = pl.pallas_call(
        spread_kernel, in_specs=[VM] * 8, out_specs=VM,
        out_shape=jax.ShapeDtypeStruct((D, D), bf16),
        scratch_shapes=[pltpu.VMEM((NZ, NY, 40, D), bf16)],
        name="spread",
    )(*o_parts)
    order = SLOTS[0] + SLOTS[1]
    back = [lax.ppermute(packed[order.index(j)], "tm", z_perm(j)) if j else packed[order.index(0)] for j in range(NZ)]
    return pl.pallas_call(
        out_kernel,
        in_specs=[SM] + [VM] * 10,
        out_specs=VM,
        out_shape=jax.ShapeDtypeStruct((ROWS, D), bf16),
        name="out",
    )(valid_count, residual, *back, o_all)


def solution(mesh):
    return jax.shard_map(
        encode,
        mesh=mesh,
        in_specs=(
            P(("seg", "tm"), None), P(), P(), P(), P(), P(), P(), P(), P(),
            P("tm", None), P("tm", None), P("seg"), P("seg"), P("seg"),
        ),
        out_specs=P(("seg", "tm"), None),
        check_vma=False,
    )
```

```python
import functools

import jax
import jax.numpy as jnp
from jax import lax
from jax.experimental import pallas as pl
from jax.experimental.pallas import tpu as pltpu
from jax.sharding import PartitionSpec as P


NY, NZ = 4, 8
ROWS = 192
GROUP = ROWS * NZ
C = 512
D = 1280
HD = 80
PAIR = 2 * HD
EPS = 1e-05
LOG2E = 1.4426950408889634
LOW = -1e30
BLOCK, KEYS = 768, 512
f32, bf16 = jnp.float32, jnp.bfloat16
VM = pl.BlockSpec(memory_space=pltpu.VMEM)
SM = pl.BlockSpec(memory_space=pltpu.SMEM)


def norm(values, gain_row):
    center = values - jnp.mean(values, axis=-1, keepdims=True)
    spread = jnp.mean(center * center, axis=-1, keepdims=True)
    return center * lax.rsqrt(spread + EPS) * gain_row


def gelu(v):
    return 0.5 * v * (1.0 + lax.erf(v * 0.7071067811865476))


def mm(a, b):
    return jnp.dot(a, b, preferred_element_type=f32)


def row(ref):
    return ref[...].reshape(1, -1)


def residual_of(normed, proj_weight, embed, starts, lengths, position, valid):
    projected = mm(normed, proj_weight)
    hit = (position >= starts) & (position < starts + lengths)
    covered = jnp.max(hit.astype(jnp.int32), axis=1, keepdims=True) > 0
    residual = jnp.where(covered, embed, projected)
    return jnp.where(position < valid, residual, 0.0)


def place():
    t = lax.axis_index("tm")
    return t // NZ, t & (NZ - 1)


def shift_of(x, c):
    return jnp.where(c == 0, x, jnp.where(x == 0, 4, NZ - x))


def pick_kernel(w_ref, ow_ref, out_ref):
    s = lax.axis_index("seg")
    target = (place()[1] - shift_of(s // 2, s & 1)) & (NZ - 1)
    out_ref[:, :D] = ow_ref[...]
    for i in range(NZ):
        @pl.when(target == i)
        def _(i=i):
            out_ref[:, D:] = jnp.concatenate(
                [w_ref[:, D * j + PAIR * i:D * j + PAIR * i + PAIR] for j in range(3)], axis=1)


def pack_kernel(*refs):
    y = place()[0]
    for k in range(NY):
        refs[NY][(y + k) & (NY - 1)] = refs[k][:, D:]
        refs[NY + 1][(y + k) & (NY - 1)] = refs[k][:, :D]


def spread(parts, hold, out_ref):
    z = place()[1]
    s = lax.axis_index("seg")
    for cross in range(2):
        for dx in range(4):
            source = (shift_of((s // 2 + dx) & 3, (s + cross) & 1) + z) & (NZ - 1)
            hold[source] = parts[cross * 4 + dx][...]
    for i in range(NY * NZ):
        out_ref[40 * i:40 * i + 40, :] = hold[i % NZ, i // NZ]


def spread_kernel(*refs):
    spread(refs[:8], refs[9], refs[8])


def conv_kernel(valid_ref, x_ref, w1_ref, g1_ref, w2_ref, g2_ref, pg_ref, pw_ref, me_ref, st_ref, ln_ref,
                normed_ref, res_ref, a_ref, b_ref):
    def pairs(inputs, w_ref, rows):
        left = mm(inputs, w_ref[:C, :])
        right = mm(inputs, w_ref[C:, :])
        parts = []
        for i in range(C // 128):
            a_ref[i, pl.ds(0, 2 * rows), :] = left[:, 128 * i:128 * i + 128]
            b_ref[i, pl.ds(0, 2 * rows), :] = right[:, 128 * i:128 * i + 128]
            parts.append(a_ref[i, pl.ds(0, rows, stride=2), :] + b_ref[i, pl.ds(1, rows, stride=2), :])
        return jnp.concatenate(parts, axis=1)

    first = gelu(norm(pairs(x_ref[...], w1_ref, 2 * ROWS), row(g1_ref))).astype(bf16)
    second = gelu(norm(pairs(first, w2_ref, ROWS), row(g2_ref))).astype(bf16)
    normed = norm(second.astype(f32), row(pg_ref)).astype(bf16)
    normed_ref[...] = normed
    position = lax.axis_index("tm") * ROWS + lax.broadcasted_iota(jnp.int32, (ROWS, 1), 0)
    res_ref[...] = residual_of(normed, pw_ref[...], row(me_ref), row(st_ref), row(ln_ref), position, valid_ref[0])


SLOTS = ((1, 7, 2, 6), (3, 5, 0, 4))


def qkv_kernel(half, count, valid_ref, pw_ref, me_ref, ag_ref, st_ref, ln_ref, *refs):
    blocks = refs[:count]
    rest = refs[count:]
    if half == 0:
        parts, (q_ref, kv_ref, ws_ref, hold) = rest[:8], rest[8:]
        spread(parts, hold, ws_ref)
    else:
        ws_ref, _, q_ref, kv_ref = rest
    block = 2 * ROWS
    y, z = place()
    rows_in = lax.broadcasted_iota(jnp.int32, (block, 1), 0)
    for p in range(2):
        ends = [((z + SLOTS[half][2 * p + i]) & (NZ - 1)) * ROWS for i in range(2)]
        position = y * GROUP + rows_in + jnp.where(rows_in < ROWS, ends[0], ends[1] - ROWS)
        inputs = jnp.concatenate([b[...] for b in blocks[2 * p:count if p else 2]], axis=0)
        residual = residual_of(inputs, pw_ref[...], row(me_ref), row(st_ref), row(ln_ref), position, valid_ref[0])
        attn_in = norm(residual, row(ag_ref)).astype(bf16)
        joined = mm(attn_in, ws_ref[...]).astype(bf16)
        scaled = joined[:, :PAIR].astype(f32) * (LOG2E * HD ** -0.5)
        hi = scaled.astype(bf16)
        lo = (scaled - hi.astype(f32)).astype(bf16)
        one = jnp.ones((block, 1), bf16)
        pad = jnp.zeros((block, 95), bf16)
        parts = []
        for h in range(2):
            parts += [hi[:, h * HD:h * HD + HD], lo[:, h * HD:h * HD + HD], one, pad]
        q_ref[block * p:block * p + block, :] = jnp.concatenate(parts, axis=1)
        kv_ref[:, block * p:block * p + block] = joined[:, PAIR:].astype(f32).T.astype(bf16)


def attend_kernel(offsets, first, last, *refs):
    count = len(offsets)
    valid_ref, q_ref = refs[:2]
    kv_refs = refs[2:2 + 2 * count]
    rest = refs[2 + 2 * count:]
    prev = None if first else rest[0]
    outs = rest[int(not first):-3]
    kk, vv, acc = rest[-3:]
    half = GROUP // 2
    valid = valid_ref[0]
    y, z = place()
    c, g = pl.program_id(0), pl.program_id(1)
    base = ((y + pick(offsets, c)) & (NY - 1)) * GROUP

    @pl.when(g == 0)
    def _():
        lane = lax.broadcasted_iota(jnp.int32, (16, half), 1)
        line = lax.broadcasted_iota(jnp.int32, (16, half), 0)
        for p in range(2):
            cols = pl.ds(half * p, half)
            spot = lane
            for i in range(4):
                shift = ((z + SLOTS[p][i]) & (NZ - 1)) * ROWS - i * ROWS
                spot = jnp.where(lane // ROWS == i, lane + shift, spot)
            bias = jnp.where((line == 0) & (base + spot >= valid), LOW, 0.0).astype(bf16)
            for h in range(2):
                kk[h, 2 * HD:2 * HD + 16, cols] = bias
                kk[h, 2 * HD + 16:, cols] = jnp.zeros((80, half), bf16)
                vv[h, HD:HD + 16, cols] = jnp.where(line == 0, 1.0, 0.0).astype(bf16)
                vv[h, HD + 16:, cols] = jnp.zeros((32, half), bf16)
            for i in range(count):
                @pl.when(c == i)
                def _(i=i, p=p, cols=cols):
                    kv = kv_refs[2 * i + p]
                    for h in range(2):
                        keys = kv[h * HD:h * HD + HD, :]
                        kk[h, 0:HD, cols] = keys
                        kk[h, HD:2 * HD, cols] = keys
                        vv[h, 0:HD, cols] = kv[PAIR + h * HD:PAIR + h * HD + HD, :]

    lane = lax.broadcasted_iota(jnp.int32, (BLOCK, 128), 1)

    @pl.when(c == 0)
    def _():
        for h in range(2):
            acc[g, h] = jnp.where(lane == HD + 1, LOW, 0.0) if first else prev[:, h * 128:h * 128 + 128]

    @pl.when(base < valid)
    def _():
        for h in range(2):
            state = acc[g, h]
            old = jnp.max(jnp.where(lane == HD + 1, state, -3e38), axis=1, keepdims=True)
            for k in range(GROUP // KEYS):
                cols = slice(k * KEYS, k * KEYS + KEYS)
                scores = mm(q_ref[:, h * 256:h * 256 + 256], kk[h, :, cols])
                peak = jnp.maximum(old, jnp.max(scores, axis=1, keepdims=True))
                weights = jnp.exp2(scores - peak).astype(bf16)
                mixed = lax.dot_general(
                    weights, vv[h, :, cols], (((1,), (1,)), ((), ())), preferred_element_type=f32)
                state = state * jnp.exp2(old - peak) + mixed
                old = peak
            acc[g, h] = jnp.where(lane == HD + 1, old, state)

    @pl.when(c == count - 1)
    def _():
        if not last:
            for h in range(2):
                outs[0][:, h * 128:h * 128 + 128] = acc[g, h]
            return
        both = jnp.concatenate([(acc[g, h] / acc[g, h][:, HD:HD + 1])[:, :HD] for h in range(2)], axis=1)
        for b in range(BLOCK // ROWS):
            rows = both[b * ROWS:b * ROWS + ROWS]
            tail = rows[:, 128:]
            head = rows[:, :128].astype(bf16)
            packed = jnp.concatenate([tail[48 * i:48 * i + 48] for i in range(4)], axis=1).astype(bf16)
            for t in range(GROUP // BLOCK):
                @pl.when(g == t)
                def _(out=outs[t * (BLOCK // ROWS) + b], head=head, packed=packed):
                    out[0:ROWS, :] = head
                    out[ROWS:, :] = packed


def pick(values, index):
    got = jnp.int32(values[0])
    for i, v in enumerate(values[1:]):
        got = jnp.where(index == i + 1, v, got)
    return got


def attend(offsets, first, last, valid, queries, chunks, state):
    count = len(offsets)
    kv_spec = pl.BlockSpec((2 * PAIR, GROUP // 2), lambda c, g: (0, 0))
    in_specs = [SM, pl.BlockSpec((BLOCK, 512), lambda c, g: (g, 0))] + [kv_spec] * (2 * count)
    args = [valid, queries] + list(chunks)
    if not first:
        in_specs.append(pl.BlockSpec((BLOCK, 256), lambda c, g: (jnp.where(c == 0, g, 1), 0)))
        args.append(state)
    if last:
        out_shape = [jax.ShapeDtypeStruct((240, 128), bf16)] * NZ
        out_spec = [pl.BlockSpec((240, 128), lambda c, g: (0, 0))] * NZ
    else:
        out_shape = jax.ShapeDtypeStruct((GROUP, 256), f32)
        out_spec = pl.BlockSpec((BLOCK, 256), lambda c, g: (jnp.where(c == count - 1, g, 0), 0))
    return pl.pallas_call(
        functools.partial(attend_kernel, offsets, first, last),
        grid=(count, GROUP // BLOCK),
        in_specs=in_specs,
        out_specs=out_spec,
        out_shape=out_shape,
        scratch_shapes=[pltpu.VMEM((2, 256, GROUP), bf16), pltpu.VMEM((2, 128, GROUP), bf16),
                        pltpu.VMEM((GROUP // BLOCK, 2, BLOCK, 128), f32)],
        cost_estimate=pl.CostEstimate(
            flops=count * 4 * GROUP * GROUP * 512, bytes_accessed=count * 2 * PAIR * GROUP * 2,
            transcendentals=count * 2 * GROUP * GROUP),
    )(*args)


def out_kernel(valid_ref, res_ref, *refs):
    m_refs, os_ref, out_ref = refs[:NZ], refs[NZ], refs[NZ + 1]
    z = place()[1]
    total = res_ref[...]
    for j in range(NZ):
        m_ref = m_refs[j]
        tail = m_ref[ROWS:, :]
        tail = jnp.concatenate([tail[:, 32 * i:32 * i + 32] for i in range(4)], axis=0)
        merged = jnp.concatenate([m_ref[:ROWS, :], tail], axis=1)
        start = pl.multiple_of(((z - j) & (NZ - 1)) * PAIR, PAIR)
        total = total + mm(merged, os_ref[pl.ds(start, PAIR), :])
    position = lax.axis_index("tm") * ROWS + lax.broadcasted_iota(jnp.int32, (ROWS, 1), 0)
    out_ref[...] = jnp.where(position < valid_ref[0], total, 0.0).astype(bf16)


def z_perm(shift):
    return [(y * NZ + z, y * NZ + (z + shift) % NZ) for y in range(NY) for z in range(NZ)]


def y_perm(shift):
    return [(y * NZ + z, ((y + shift) % NY) * NZ + z) for y in range(NY) for z in range(NZ)]


def seg_perm(shift):
    return [(s, (s + shift) % 8) for s in range(8)]


def fetch_perm():
    shift = lambda s: s // 2 if s % 2 == 0 else (NZ - s // 2 if s > 1 else 4)
    return [
        (s * 32 + y * NZ + (z + shift(s)) % NZ, s * 32 + y * NZ + z)
        for s in range(8) for y in range(NY) for z in range(NZ)
    ]


def share(got):
    mine = [got] + [lax.ppermute(got, "seg", seg_perm(-2 * d)) for d in range(1, 4)]
    return mine + [lax.ppermute(m, "seg", [(s, s ^ 1) for s in range(8)]) for m in mine]


def encode(frames, conv1_weight, conv1_gain, conv2_weight, conv2_gain, proj_gain, proj_weight, mask_embed,
           attn_gain, qkv_weight, out_weight, span_starts, span_lengths, valid_count):
    columns = pl.pallas_call(
        pick_kernel, in_specs=[VM, VM], out_specs=VM,
        out_shape=jax.ShapeDtypeStruct((40, D + 3 * PAIR), bf16), name="pick",
    )(qkv_weight, out_weight)
    fetched = lax.ppermute(columns, ("seg", "tm"), fetch_perm())
    near = [fetched] + [lax.ppermute(fetched, "tm", y_perm(-k)) for k in range(1, NY)]
    w_pack, o_pack = pl.pallas_call(
        pack_kernel, in_specs=[VM] * NY, out_specs=(VM, VM),
        out_shape=(jax.ShapeDtypeStruct((NY, 40, 3 * PAIR), bf16), jax.ShapeDtypeStruct((NY, 40, D), bf16)),
        name="pack",
    )(*near)
    w_parts = share(w_pack)

    normed, residual = pl.pallas_call(
        conv_kernel,
        in_specs=[SM] + [VM] * 10,
        out_specs=(VM, VM),
        out_shape=(jax.ShapeDtypeStruct((ROWS, C), bf16), jax.ShapeDtypeStruct((ROWS, D), f32)),
        scratch_shapes=[pltpu.VMEM((C // 128, 4 * ROWS, 128), f32)] * 2,
        cost_estimate=pl.CostEstimate(flops=4 * 10**9, bytes_accessed=6 * 10**6, transcendentals=0),
        name="conv",
    )(valid_count, frames, conv1_weight, conv1_gain, conv2_weight, conv2_gain, proj_gain, proj_weight,
      mask_embed, span_starts, span_lengths)

    up, down = [normed], [normed]
    for _ in range(3):
        up.append(lax.ppermute(up[-1], "tm", z_perm(-1)))
        down.append(lax.ppermute(down[-1], "tm", z_perm(1)))
    half = ROWS // 2
    far = [lax.ppermute(down[3][:half], "tm", z_perm(1)), lax.ppermute(up[3][half:], "tm", z_perm(-1))]

    shared = (valid_count, proj_weight, mask_embed, attn_gain, span_starts, span_lengths)
    q_shape = jax.ShapeDtypeStruct((GROUP, 512), bf16)
    kv_shape = jax.ShapeDtypeStruct((2 * PAIR, GROUP // 2), bf16)
    w_shape = jax.ShapeDtypeStruct((D, 3 * PAIR), bf16)
    q_spec = [pl.BlockSpec((GROUP // 2, 512), functools.partial(lambda h, i: (h, 0), h)) for h in range(2)]
    cost = pl.CostEstimate(flops=8 * 10**9, bytes_accessed=4 * 10**6, transcendentals=0)
    queries, kv_a, w_all = pl.pallas_call(
        functools.partial(qkv_kernel, 0, 4),
        grid=(1,),
        in_specs=[SM] + [VM] * 17,
        out_specs=(q_spec[0], VM, VM),
        out_shape=(q_shape, kv_shape, w_shape),
        scratch_shapes=[pltpu.VMEM((NZ, NY, 40, 3 * PAIR), bf16)],
        cost_estimate=cost,
        name="qkv0",
    )(*shared, up[1], down[1], up[2], down[2], *w_parts)
    queries, kv_b = pl.pallas_call(
        functools.partial(qkv_kernel, 1, 5),
        grid=(1,),
        in_specs=[SM] + [VM] * 11 + [pl.BlockSpec(memory_space=pl.ANY)],
        out_specs=(q_spec[1], VM),
        out_shape=(q_shape, kv_shape),
        input_output_aliases={12: 0},
        cost_estimate=cost,
        name="qkv1",
    )(*shared, up[3], down[3], normed, *far, w_all, queries)

    ahead = [lax.ppermute(kv, "tm", y_perm(-1)) for kv in (kv_a, kv_b)]
    behind = [lax.ppermute(kv, "tm", y_perm(1)) for kv in (kv_a, kv_b)]
    across = [lax.ppermute(ahead[0], "tm", y_perm(-1)), lax.ppermute(behind[1], "tm", y_perm(1))]
    o_parts = share(lax.optimization_barrier((o_pack, kv_b))[0])
    state = attend((0,), True, False, valid_count, queries, (kv_a, kv_b), None)
    state = attend((1, 3), False, False, valid_count, queries, ahead + behind, state)
    packed = list(attend((2,), False, True, valid_count, queries, across, state))
    *o_parts, packed[0] = lax.optimization_barrier((*o_parts, packed[0]))
    o_all = pl.pallas_call(
        spread_kernel, in_specs=[VM] * 8, out_specs=VM,
        out_shape=jax.ShapeDtypeStruct((D, D), bf16),
        scratch_shapes=[pltpu.VMEM((NZ, NY, 40, D), bf16)],
        name="spread",
    )(*o_parts)
    order = SLOTS[0] + SLOTS[1]
    back = [lax.ppermute(packed[order.index(j)], "tm", z_perm(j)) if j else packed[order.index(0)] for j in range(NZ)]
    return pl.pallas_call(
        out_kernel,
        in_specs=[SM] + [VM] * 10,
        out_specs=VM,
        out_shape=jax.ShapeDtypeStruct((ROWS, D), bf16),
        name="out",
    )(valid_count, residual, *back, o_all)


def solution(mesh):
    return jax.shard_map(
        encode,
        mesh=mesh,
        in_specs=(
            P(("seg", "tm"), None), P(), P(), P(), P(), P(), P(), P(), P(),
            P("tm", None), P("tm", None), P("seg"), P("seg"), P("seg"),
        ),
        out_specs=P(("seg", "tm"), None),
        check_vma=False,
    )
```
